32 devices in a mesh: layer: 4 (over y, core), feat: 4 (over z), path: 2 (over x).
Axes of the slice: x: 2, y: 2, z: 4, core: 2. Of those that a mesh axis runs over, the one named last changes fastest.
Arguments:
- context: bfloat16 [4, 64, 2304], P('layer'), may hold values from -6 to 6
- targets: bfloat16 [4, 64, 2304], P('layer'), may hold values from -4 to 4
- beyond_targets: bfloat16 [64, 2304], replicated, may hold values from -4 to 4
- positions: int32 [32], replicated, may hold values from 0 to 63
- donors: int32 [32], replicated, may hold values from 0 to 63
- encoder: bfloat16 [4, 2304, 8192], P('layer', None, 'feat'), may hold values from -0.125 to 0.125
- encoder_bias: float32 [4, 8192], P('layer', 'feat'), may hold values from -3 to 3
- decoder: bfloat16 [4, 2, 8192, 2304], P('layer', None, 'feat', 'path'), may hold values from -0.0625 to 0.0625
Outputs:
- attribution: float32 [4, 32, 2304], P('layer', None, ('feat', 'path'))
The draws below stay inside these ranges and needn't reach their ends.
All inputs are finite; a program needn't handle non-finite values.
Results may differ from the reference program's by a relative error of at most 0.0071.
Values may be sent and summed in bfloat16 or wider, within the bound.
A program may use at most 64 MiB of HBM per device.

```python
import jax
import jax.numpy as jnp

D = 2304
F = 8192
LAYERS = 4
ROWS_PT = 32
CTX = 64
PTS_DEV = 4
N_PATH = 2


def with_ends(drawn, key, least, top_value):
    longest = drawn.shape.index(max(drawn.shape))
    spots = []
    for shift in (0, 1):
        where = [jax.random.randint(jax.random.fold_in(key, axis), (), 0, length) for axis, length in enumerate(drawn.shape)]
        where[longest] = (where[longest] + shift) % drawn.shape[longest]
        spots.append(tuple(where))
    return drawn.at[spots[0]].set(least).at[spots[1]].set(top_value)


def levels(rng, extent, cuts, smallest, largest):
    loudness = 1.0
    for dim, blocks in cuts:
        draws = jax.random.uniform(jax.random.fold_in(jax.random.fold_in(rng, 6), dim), (blocks,), jnp.float32, smallest / len(cuts), largest / len(cuts))
        loudness = loudness * jnp.repeat(jnp.exp(draws), extent[dim] // blocks).reshape((-1,) + (1,) * (len(extent) - 1 - dim))
    return loudness


def noise(own_key, extent, spread, limit, split=(), kind=jnp.bfloat16):
    drawn = spread * jax.random.normal(own_key, extent, jnp.float32)
    if split:
        drawn = drawn * levels(own_key, extent, split, -0.22, 0.18)
    return jnp.clip(drawn, -limit, limit).astype(kind)


def setup_inputs(seed: int = 0) -> dict:
    streams_of = jax.random.split(jax.random.key(seed), 9)
    context = noise(streams_of[0], (LAYERS, CTX, D), 1.0, 6.0, ((0, 4),))
    targets = noise(streams_of[1], (LAYERS, CTX, D), 0.5, 4.0, ((0, 4),))
    beyond_targets = noise(streams_of[2], (CTX, D), 0.5, 4.0)
    positions = with_ends(jax.random.randint(streams_of[3], (ROWS_PT,), 0, CTX), jax.random.fold_in(streams_of[3], 1), 0, CTX - 1).astype(jnp.int32)
    donors = with_ends(jax.random.randint(streams_of[4], (ROWS_PT,), 0, CTX), jax.random.fold_in(streams_of[4], 1), 0, CTX - 1).astype(jnp.int32)
    encoder = noise(streams_of[5], (LAYERS, D, F), D ** -0.5, 0.125, ((0, 4), (2, 4)))
    encoder_bias = noise(streams_of[6], (LAYERS, F), 0.5, 3.0, ((0, 4), (1, 4)), jnp.float32)
    decoder = noise(streams_of[7], (LAYERS, 2, F, D), F ** -0.5, 0.0625, ((0, 4), (2, 4), (3, 2)))
    return {"context": context, "targets": targets, "beyond_targets": beyond_targets, "positions": positions, "donors": donors, "encoder": encoder, "encoder_bias": encoder_bias, "decoder": decoder}


def reference(context, targets, beyond_targets, positions, donors, encoder, encoder_bias, decoder):
    points = PTS_DEV * N_PATH
    fraction = (jnp.arange(points).astype(jnp.float32) + 0.5) / points
    offsets = []
    preacts = []
    parts = []
    for source in range(LAYERS):
        source_rows = context[source][positions].astype(jnp.float32)
        donor_rows = context[source][donors].astype(jnp.float32)
        offset = source_rows - donor_rows
        inputs = (donor_rows[None] + fraction[:, None, None] * offset[None]).astype(jnp.bfloat16).reshape(-1, D)
        preact = jnp.dot(inputs, encoder[source], preferred_element_type=jnp.float32) + encoder_bias[source]
        code_rows = jnp.maximum(preact, 0.0).astype(jnp.bfloat16)
        here = jnp.dot(code_rows, decoder[source, 0], preferred_element_type=jnp.float32)
        later = jnp.dot(code_rows, decoder[source, 1], preferred_element_type=jnp.float32)
        offsets.append(offset)
        preacts.append(preact)
        parts.append((here, later))
    errors = []
    for target in range(LAYERS + 1):
        if target == LAYERS:
            rebuilt = parts[LAYERS - 1][1]
            goal_rows = beyond_targets[positions].astype(jnp.float32)
        else:
            rebuilt = parts[target][0]
            if target > 0:
                rebuilt = rebuilt + parts[target - 1][1]
            goal_rows = targets[target][positions].astype(jnp.float32)
        rebuilt = rebuilt.reshape(points, ROWS_PT, D)
        errors.append((rebuilt - goal_rows[None]).astype(jnp.bfloat16).reshape(-1, D))
    results = []
    for source in range(LAYERS):
        grads = jnp.dot(errors[source], decoder[source, 0].T, preferred_element_type=jnp.float32)
        grads = grads + jnp.dot(errors[source + 1], decoder[source, 1].T, preferred_element_type=jnp.float32)
        gated = jnp.where(preacts[source] > 0, grads, 0.0).astype(jnp.bfloat16)
        input_grads = jnp.dot(gated, encoder[source].T, preferred_element_type=jnp.float32)
        summed = input_grads.reshape(points, ROWS_PT, D).sum(axis=0)
        results.append(offsets[source] * summed / points)
    return jnp.stack(results)
```

```python
import functools

import jax
import jax.numpy as jnp
from jax import lax
from jax.experimental import pallas as pl
from jax.experimental.pallas import tpu as pltpu
from jax.sharding import PartitionSpec as P

PTS_DEV = 4
CHUNKS = 8
MESH = pl.DeviceIdType.MESH
NT = (((1,), (1,)), ((), ()))


def tile_of(width, most):
    sizes = [t for t in range(128, most + 1, 128) if width % t == 0]
    return sizes[-1] if sizes else width


def aligned(start, size):
    return pl.ds(pl.multiple_of(start, size), size)


def kernel(
    shape, pos_ref, don_ref, ctx_ref, tgt_ref, bey_ref, bias_ref, ctxb_ref, enc_hbm, dec_hbm, out_ref,
    enc, dec, inputs, codes, own, later, later_in, goal, red_recv, red_send, err, gsum, part, final_send, final_recv,
    enc_sem, dec_sem, later_sem, red_sem, err_sem, next_sem, final_sem,
):
    layers, n, paths = shape
    layer, z, path = lax.axis_index("layer"), lax.axis_index("feat"), lax.axis_index("path")
    last = layers - 1
    height, tokens = pos_ref.shape[0], ctx_ref.shape[0]
    rows, width = inputs.shape
    feats, cols = codes.shape[1], own.shape[1]
    points = rows // height
    half = rows // 2
    chunk = half // CHUNKS
    groups = n * paths
    me = z * paths + path
    scatter = final_send is not None

    barrier = pltpu.get_barrier_semaphore()

    def greet(i, carry):
        other = lax.rem(me + 1 + i, groups)
        pl.semaphore_signal(
            barrier, inc=1, device_id={"feat": other // paths, "path": lax.rem(other, paths)}, device_id_type=MESH
        )
        return carry

    lax.fori_loop(0, groups - 1, greet, 0)

    @pl.when(layer > 0)
    def _():
        pl.semaphore_signal(barrier, inc=1, device_id={"layer": layer - 1}, device_id_type=MESH)

    @pl.when(layer < last)
    def _():
        pl.semaphore_signal(barrier, inc=1, device_id={"layer": layer + 1}, device_id_type=MESH)

    ftile = tile_of(feats, 256)
    ftiles = feats // ftile

    def enc_copy(j):
        return pltpu.make_async_copy(
            enc_hbm.at[0, :, aligned(j * ftile, ftile)], enc.at[:, aligned(j * ftile, ftile)], enc_sem.at[j]
        )

    def dec_copy(k):
        return pltpu.make_async_copy(dec_hbm.at[0, k], dec.at[k], dec_sem.at[k])

    for j in range(ftiles):
        enc_copy(j).start()
    dec_copy(1).start()
    dec_copy(0).start()

    token = lax.broadcasted_iota(jnp.int32, (height, tokens), 1)
    pick_source = (token == pos_ref[...]).astype(jnp.float32).astype(jnp.bfloat16)
    pick_donor = (token == don_ref[...]).astype(jnp.float32).astype(jnp.bfloat16)

    def pick(which, ref):
        return jnp.dot(which, ref[...], preferred_element_type=jnp.float32)

    donor = pick(pick_donor, ctx_ref)
    offset = pick(pick_source, ctx_ref) - donor
    for p in range(points):
        inputs[p * height : (p + 1) * height, :] = (donor + ((p + 0.5) / points) * offset).astype(jnp.bfloat16)
    goals = (pick(pick_source, tgt_ref).astype(jnp.bfloat16), pick(pick_source, bey_ref).astype(jnp.bfloat16))
    for p in range(points):
        for k in (0, 1):
            goal[k, p * height : (p + 1) * height, :] = goals[k]

    @pl.when(layer == 0)
    def _():
        later_in[...] = jnp.zeros_like(later_in)

    def encode(j, carry):
        enc_copy(j).wait()
        at = aligned(j * ftile, ftile)
        preact = jnp.dot(inputs[...], enc[:, at], preferred_element_type=jnp.float32) + bias_ref[:, at]
        codes[:, at] = jnp.maximum(preact, 0.0).astype(jnp.bfloat16)
        return carry

    lax.fori_loop(0, ftiles, encode, 0)

    ctile = tile_of(cols, 384)

    def decode(k, into):
        def step(j, carry):
            at = aligned(j * ctile, ctile) if cols > ctile else slice(None)
            value = jnp.dot(codes[...], dec[k, :, at], preferred_element_type=jnp.float32)
            into[:, at] = value.astype(into.dtype)
            return carry

        dec_copy(k).wait()
        lax.fori_loop(0, cols // ctile, step, 0)

    decode(1, later)

    pl.semaphore_wait(barrier, groups - 1 + jnp.minimum(layer, 1) + jnp.minimum(last - layer, 1))

    def at_rows(d, c):
        return aligned(d * half + c * chunk, chunk)

    def later_copy(d, c):
        at = at_rows(d, c)
        return pltpu.make_async_remote_copy(
            later.at[at, :], later_in.at[at, :], later_sem.at[0, d, c], later_sem.at[1, d, c],
            device_id={"layer": lax.rem(layer + 1, layers)}, device_id_type=MESH,
        )

    def place(d):
        return (n - 1 - z, z - 1, z + 1) if d == 0 else (z, z + 1, z - 1)

    def wrap(i):
        return lax.rem(i + n, n)

    def red_copy(k, d, c):
        at = at_rows(d, c)
        return pltpu.make_async_remote_copy(
            red_send.at[k, at, :], red_recv.at[k, at, :], red_sem.at[0, k, d, c], red_sem.at[1, k, d, c],
            device_id={"feat": wrap(place(d)[1])}, device_id_type=MESH,
        )

    def err_copy(k, d, c):
        at = at_rows(d, c)
        return pltpu.make_async_remote_copy(
            err.at[k, at, :], err.at[k, at, :], err_sem.at[0, k, d, c], err_sem.at[1, k, d, c],
            device_id={"feat": wrap(place(d)[2])}, device_id_type=MESH,
        )

    def next_copy(d, c):
        at = at_rows(d, c)
        return pltpu.make_async_remote_copy(
            err.at[0, at, :], err.at[1, at, :], next_sem.at[0, d, c], next_sem.at[1, d, c],
            device_id={"layer": lax.rem(layer + last, layers)}, device_id_type=MESH,
        )

    def each_chunk(act):
        def step(c, carry):
            for d in (0, 1):
                act(d, c)
            return carry

        lax.fori_loop(0, CHUNKS, step, 0)

    @pl.when(layer < last)
    def _():
        each_chunk(lambda d, c: later_copy(d, c).start())

    decode(0, own)

    def hand_on(k, d, c):
        @pl.when(place(d)[0] > 0)
        def _():
            err_copy(k, d, c).start()

        if k == 0:

            @pl.when(layer > 0)
            def _():
                next_copy(d, c).start()

    def reduce_step(k, d, c):
        at = at_rows(d, c)
        position = place(d)[0]

        def base():
            if k == 1:
                return later[at, :].astype(jnp.float32)
            return own[at, :] + later_in[at, :].astype(jnp.float32)

        if k == 0:

            @pl.when(layer > 0)
            def _():
                later_copy(d, c).wait_recv()

        @pl.when(position == 0)
        def _():
            red_send[k, at, :] = base().astype(jnp.bfloat16)
            red_copy(k, d, c).start()

        @pl.when(position > 0)
        def _():
            red_copy(k, d, c).wait_recv()

            @pl.when(position < n - 1)
            def _():
                red_send[k, at, :] = (base() + red_recv[k, at, :].astype(jnp.float32)).astype(jnp.bfloat16)
                red_copy(k, d, c).start()

            @pl.when(position == n - 1)
            def _():
                rebuilt = base() + red_recv[k, at, :].astype(jnp.float32)
                err[k, at, :] = (rebuilt - goal[k, at, :].astype(jnp.float32)).astype(jnp.bfloat16)
                hand_on(k, d, c)

    def gather_step(k, d, c):
        err_copy(k, d, c).wait_recv()
        hand_on(k, d, c)

    def on_chains(act, d, c):
        act(0, d, c)

        @pl.when(layer == last)
        def _():
            act(1, d, c)

    def chain(t, carry):
        for d in (0, 1):
            position = place(d)[0]
            c = t - position

            @pl.when((c >= 0) & (c < CHUNKS))
            def _():
                on_chains(reduce_step, d, c)

            g = t - (2 * (n - 1) - position)

            @pl.when((position < n - 1) & (g >= 0) & (g < CHUNKS))
            def _():
                on_chains(gather_step, d, g)

        return carry

    lax.fori_loop(0, CHUNKS + 2 * (n - 1), chain, 0)

    @pl.when(layer < last)
    def _():
        each_chunk(lambda d, c: next_copy(d, c).wait_recv())

    def grads_step(j, carry):
        at = aligned(j * ftile, ftile)
        grads = lax.dot_general(err[0], dec[0, at, :], NT, preferred_element_type=jnp.float32)
        grads = grads + lax.dot_general(err[1], dec[1, at, :], NT, preferred_element_type=jnp.float32)
        gated = jnp.where(codes[:, at].astype(jnp.float32) > 0, grads, 0.0)
        gsum[:, at] = gated.reshape(points, height, ftile).sum(axis=0).astype(jnp.bfloat16)
        return carry

    lax.fori_loop(0, ftiles, grads_step, 0)

    if scatter:
        block = width // groups

        def final_copy(sender, target):
            return pltpu.make_async_remote_copy(
                final_send.at[target], final_recv.at[sender], final_sem.at[0, target], final_sem.at[1, sender],
                device_id={"feat": target // paths, "path": lax.rem(target, paths)}, device_id_type=MESH,
            )

        def product(b):
            return lax.dot_general(gsum[...], enc[aligned(b * block, block), :], NT, preferred_element_type=jnp.float32)

        def send_block(i, carry):
            b = lax.rem(me + 1 + i, groups)
            final_send[b] = product(b).astype(jnp.bfloat16)
            final_copy(me, b).start()
            return carry

        lax.fori_loop(0, groups - 1, send_block, 0)
        part[...] = product(me)

        def take_block(i, carry):
            b = lax.rem(me + 1 + i, groups)
            final_copy(b, b).wait_recv()
            part[...] += final_recv[b].astype(jnp.float32)
            return carry

        lax.fori_loop(0, groups - 1, take_block, 0)
        offset_here = pick(pick_source, ctxb_ref) - pick(pick_donor, ctxb_ref)
        out_ref[...] = offset_here * part[...] / points

        def sent_block(i, carry):
            b = lax.rem(me + 1 + i, groups)
            final_copy(me, b).wait_send()
            return carry

        lax.fori_loop(0, groups - 1, sent_block, 0)
    else:
        out_ref[...] = lax.dot_general(gsum[...], enc[...], NT, preferred_element_type=jnp.float32)

    def sent(d, c):
        position = place(d)[0]

        def of_chain(k, d, c):
            @pl.when(position < n - 1)
            def _():
                red_copy(k, d, c).wait_send()

            @pl.when(position > 0)
            def _():
                err_copy(k, d, c).wait_send()

        @pl.when(layer < last)
        def _():
            later_copy(d, c).wait_send()

        on_chains(of_chain, d, c)

        @pl.when(layer > 0)
        def _():
            next_copy(d, c).wait_send()

    each_chunk(sent)


def per_device(shape, context, targets, beyond_targets, positions, donors, encoder, encoder_bias, decoder):
    layers, n, paths = shape
    path = lax.axis_index("path")
    height = positions.shape[0]
    width, feats = encoder.shape[1:]
    cols = decoder.shape[3]
    points = PTS_DEV * paths
    rows = points * height
    groups = n * paths
    block = width // groups
    me = lax.axis_index("feat") * paths + path
    scatter = block % 16 == 0
    ctx = context[0]
    tgt = lax.dynamic_slice_in_dim(targets[0], path * cols, cols, 1)
    bey = lax.dynamic_slice_in_dim(beyond_targets, path * cols, cols, 1)
    ctxb = lax.dynamic_slice_in_dim(ctx, me * block, block, 1)
    bf16, f32 = jnp.bfloat16, jnp.float32
    dma = pltpu.SemaphoreType.DMA
    final = (
        [
            pltpu.VMEM((height, block), f32),
            pltpu.VMEM((groups, height, block), bf16),
            pltpu.VMEM((groups, height, block), bf16),
        ]
        if scatter
        else [None, None, None]
    )
    scratch = [
        pltpu.VMEM((width, feats), bf16),
        pltpu.VMEM((2, feats, cols), bf16),
        pltpu.VMEM((rows, width), bf16),
        pltpu.VMEM((rows, feats), bf16),
        pltpu.VMEM((rows, cols), f32),
        pltpu.VMEM((rows, cols), bf16),
        pltpu.VMEM((rows, cols), bf16),
        pltpu.VMEM((2, rows, cols), bf16),
        pltpu.VMEM((2, rows, cols), bf16),
        pltpu.VMEM((2, rows, cols), bf16),
        pltpu.VMEM((2, rows, cols), bf16),
        pltpu.VMEM((height, feats), bf16),
        *final,
        dma((feats // tile_of(feats, 256),)),
        dma((2,)),
        dma((2, 2, CHUNKS)),
        dma((2, 2, 2, CHUNKS)),
        dma((2, 2, 2, CHUNKS)),
        dma((2, 2, CHUNKS)),
        dma((2, groups)) if scatter else None,
    ]
    kept = [s is not None for s in scratch]

    def body(*refs):
        fixed, given = refs[:10], iter(refs[10:])
        kernel(shape, *fixed, *[next(given) if k else None for k in kept])

    vmem, anywhere = pl.BlockSpec(memory_space=pltpu.VMEM), pl.BlockSpec(memory_space=pl.ANY)
    out = pl.pallas_call(
        body,
        out_shape=jax.ShapeDtypeStruct((height, block if scatter else width), f32),
        in_specs=[vmem] * 7 + [anywhere] * 2,
        out_specs=vmem,
        scratch_shapes=[s for s in scratch if s is not None],
        compiler_params=pltpu.CompilerParams(
            collective_id=0, has_side_effects=True, vmem_limit_bytes=60 * 1024 * 1024
        ),
        name="attribution",
    )(positions[:, None], donors[:, None], ctx, tgt, bey, encoder_bias, ctxb, encoder, decoder)
    if not scatter:
        quadrature = lax.psum_scatter(out, ("feat", "path"), scatter_dimension=1, tiled=True)
        offset = ctxb[positions].astype(f32) - ctxb[donors].astype(f32)
        out = offset * quadrature / points
    return out[None]


def solution(mesh):
    shape = tuple(mesh.shape[a] for a in ("layer", "feat", "path"))
    placed = (
        P("layer", None, None),
        P("layer", None, None),
        P(),
        P(),
        P(),
        P("layer", None, "feat"),
        P("layer", "feat"),
        P("layer", None, "feat", "path"),
    )
    return jax.shard_map(
        functools.partial(per_device, shape),
        mesh=mesh,
        in_specs=placed,
        out_specs=P("layer", None, ("feat", "path")),
        check_vma=False,
    )
```

```python
import functools

import jax
import jax.numpy as jnp
from jax import lax
from jax.experimental import pallas as pl
from jax.experimental.pallas import tpu as pltpu
from jax.sharding import PartitionSpec as P

PTS_DEV = 4
CHUNKS = 8
SKEW = 4
MESH = pl.DeviceIdType.MESH
NT = (((1,), (1,)), ((), ()))


def tile_of(width, most):
    sizes = [t for t in range(128, most + 1, 128) if width % t == 0]
    return sizes[-1] if sizes else width


def aligned(start, size):
    return pl.ds(pl.multiple_of(start, size), size)


def kernel(
    shape, pos_ref, don_ref, ctx_ref, tgt_ref, bey_ref, bias_ref, enc_hbm, dec_hbm, out_ref,
    enc, dec, inputs, codes, own, later, later_in, goal, red_recv, red_send, err, gsum, part, offsets, final_send, final_recv,
    enc_sem, dec_sem, later_sem, red_sem, err_sem, next_sem, final_sem,
):
    layers, n, paths = shape
    layer, z, path = lax.axis_index("layer"), lax.axis_index("feat"), lax.axis_index("path")
    last = layers - 1
    height, tokens = pos_ref.shape[1], ctx_ref.shape[1]
    rows, width = inputs.shape
    feats, cols = codes.shape[1], own.shape[1]
    points = rows // height
    half = rows // 2
    chunk = half // CHUNKS
    groups = n * paths
    me = z * paths + path
    scatter = final_send is not None

    barrier = pltpu.get_barrier_semaphore()

    def greet(i, carry):
        other = lax.rem(me + 1 + i, groups)
        pl.semaphore_signal(
            barrier, inc=1, device_id={"feat": other // paths, "path": lax.rem(other, paths)}, device_id_type=MESH
        )
        return carry

    lax.fori_loop(0, groups - 1, greet, 0)

    @pl.when(layer > 0)
    def _():
        pl.semaphore_signal(barrier, inc=1, device_id={"layer": layer - 1}, device_id_type=MESH)

    @pl.when(layer < last)
    def _():
        pl.semaphore_signal(barrier, inc=1, device_id={"layer": layer + 1}, device_id_type=MESH)

    ftile = tile_of(feats, 256)
    ftiles = feats // ftile

    def enc_copy(j):
        return pltpu.make_async_copy(
            enc_hbm.at[0, :, aligned(j * ftile, ftile)], enc.at[:, aligned(j * ftile, ftile)], enc_sem.at[j]
        )

    def dec_copy(k):
        return pltpu.make_async_copy(dec_hbm.at[0, k], dec.at[k], dec_sem.at[k])

    for j in range(ftiles):
        enc_copy(j).start()
    dec_copy(1).start()
    dec_copy(0).start()

    token = lax.broadcasted_iota(jnp.int32, (tokens, height), 0)
    pick_source = (token == pos_ref[...]).astype(jnp.float32).T.astype(jnp.bfloat16)
    pick_donor = (token == don_ref[...]).astype(jnp.float32).T.astype(jnp.bfloat16)

    def pick(which, table):
        return jnp.dot(which, table, preferred_element_type=jnp.float32)

    donor = pick(pick_donor, ctx_ref[0])
    offset = pick(pick_source, ctx_ref[0]) - donor
    for p in range(points):
        inputs[p * height : (p + 1) * height, :] = (donor + ((p + 0.5) / points) * offset).astype(jnp.bfloat16)
    @pl.when(layer == 0)
    def _():
        later_in[...] = jnp.zeros_like(later_in)

    def encode(j, carry):
        enc_copy(j).wait()
        at = aligned(j * ftile, ftile)
        preact = jnp.dot(inputs[...], enc[:, at], preferred_element_type=jnp.float32) + bias_ref[:, at]
        codes[:, at] = jnp.maximum(preact, 0.0).astype(jnp.bfloat16)
        return carry

    lax.fori_loop(0, ftiles, encode, 0)

    ctile = tile_of(cols, 384)

    def decode(k, into):
        def step(j, carry):
            at = aligned(j * ctile, ctile) if cols > ctile else slice(None)
            value = jnp.dot(codes[...], dec[k, :, at], preferred_element_type=jnp.float32)
            into[:, at] = value.astype(into.dtype)
            return carry

        dec_copy(k).wait()
        lax.fori_loop(0, cols // ctile, step, 0)

    decode(1, later)

    pl.semaphore_wait(barrier, groups - 1 + jnp.minimum(layer, 1) + jnp.minimum(last - layer, 1))

    def at_rows(d, c):
        return aligned(d * half + c * chunk, chunk)

    def later_copy(d, c):
        at = at_rows(d, c)
        return pltpu.make_async_remote_copy(
            later.at[at, :], later_in.at[at, :], later_sem.at[0, d, c], later_sem.at[1, d, c],
            device_id={"layer": lax.rem(layer + 1, layers)}, device_id_type=MESH,
        )

    def place(d):
        return (n - 1 - z, z - 1, z + 1) if d == 0 else (z, z + 1, z - 1)

    def wrap(i):
        return lax.rem(i + n, n)

    def red_copy(k, d, c):
        at = at_rows(d, c)
        return pltpu.make_async_remote_copy(
            red_send.at[k, at, :], red_recv.at[k, at, :], red_sem.at[0, k, d, c], red_sem.at[1, k, d, c],
            device_id={"feat": wrap(place(d)[1])}, device_id_type=MESH,
        )

    def err_copy(k, d, c):
        at = at_rows(d, c)
        return pltpu.make_async_remote_copy(
            err.at[k, at, :], err.at[k, at, :], err_sem.at[0, k, d, c], err_sem.at[1, k, d, c],
            device_id={"feat": wrap(place(d)[2])}, device_id_type=MESH,
        )

    def next_copy(d, c):
        at = at_rows(d, c)
        return pltpu.make_async_remote_copy(
            err.at[0, at, :], err.at[1, at, :], next_sem.at[0, d, c], next_sem.at[1, d, c],
            device_id={"layer": lax.rem(layer + last, layers)}, device_id_type=MESH,
        )

    def each_chunk(act):
        def step(c, carry):
            for d in (0, 1):
                act(d, c)
            return carry

        lax.fori_loop(0, CHUNKS, step, 0)

    @pl.when(layer < last)
    def _():
        each_chunk(lambda d, c: later_copy(d, c).start())

    decode(0, own)

    if tgt_ref.shape[2] == cols:
        goal_at = slice(None)
    else:
        goal_at = aligned(path * cols, cols)
    goals = [pick(pick_source, table).astype(jnp.bfloat16) for table in (tgt_ref[0, :, goal_at], bey_ref[:, goal_at])]
    for p in range(points):
        for k in (0, 1):
            goal[k, p * height : (p + 1) * height, :] = goals[k]
    if scatter:
        block = width // groups
        for b in range(groups):
            offsets[b] = offset[:, b * block : (b + 1) * block]

    def hand_on(k, d, c):
        @pl.when(place(d)[0] > 0)
        def _():
            err_copy(k, d, c).start()

        if k == 0:

            @pl.when(layer > 0)
            def _():
                next_copy(d, c).start()

    def reduce_step(k, d, c):
        at = at_rows(d, c)
        position = place(d)[0]

        def base():
            if k == 1:
                return later[at, :].astype(jnp.float32)
            return own[at, :] + later_in[at, :].astype(jnp.float32)

        if k == 0:

            @pl.when(layer > 0)
            def _():
                later_copy(d, c).wait_recv()

        @pl.when(position == 0)
        def _():
            red_send[k, at, :] = base().astype(jnp.bfloat16)
            red_copy(k, d, c).start()

        @pl.when(position > 0)
        def _():
            red_copy(k, d, c).wait_recv()

            @pl.when(position < n - 1)
            def _():
                red_send[k, at, :] = (base() + red_recv[k, at, :].astype(jnp.float32)).astype(jnp.bfloat16)
                red_copy(k, d, c).start()

            @pl.when(position == n - 1)
            def _():
                rebuilt = base() + red_recv[k, at, :].astype(jnp.float32)
                err[k, at, :] = (rebuilt - goal[k, at, :].astype(jnp.float32)).astype(jnp.bfloat16)
                hand_on(k, d, c)

    def gather_step(k, d, c):
        err_copy(k, d, c).wait_recv()
        hand_on(k, d, c)

    def on_chains(act, d, c):
        act(0, d, c)

        @pl.when(layer == last)
        def _():
            act(1, d, c)

    def chain(t, carry):
        for d in (0, 1):
            position = place(d)[0]
            c = t - SKEW * position

            @pl.when((c >= 0) & (c < CHUNKS))
            def _():
                on_chains(reduce_step, d, c)

            g = t - SKEW * (2 * (n - 1) - position)

            @pl.when((position < n - 1) & (g >= 0) & (g < CHUNKS))
            def _():
                on_chains(gather_step, d, g)

        return carry

    lax.fori_loop(0, CHUNKS + SKEW * 2 * (n - 1), chain, 0)

    @pl.when(layer < last)
    def _():
        each_chunk(lambda d, c: next_copy(d, c).wait_recv())

    def grads_step(j, carry):
        at = aligned(j * ftile, ftile)
        grads = lax.dot_general(err[0], dec[0, at, :], NT, preferred_element_type=jnp.float32)
        grads = grads + lax.dot_general(err[1], dec[1, at, :], NT, preferred_element_type=jnp.float32)
        gated = jnp.where(codes[:, at].astype(jnp.float32) > 0, grads, 0.0)
        gsum[:, at] = gated.reshape(points, height, ftile).sum(axis=0).astype(jnp.bfloat16)
        return carry

    lax.fori_loop(0, ftiles, grads_step, 0)

    if scatter:

        def final_copy(sender, target):
            return pltpu.make_async_remote_copy(
                final_send.at[target], final_recv.at[sender], final_sem.at[0, target], final_sem.at[1, sender],
                device_id={"feat": target // paths, "path": lax.rem(target, paths)}, device_id_type=MESH,
            )

        def product(b):
            return lax.dot_general(gsum[...], enc[aligned(b * block, block), :], NT, preferred_element_type=jnp.float32)

        def send_block(i, carry):
            b = lax.rem(me + 1 + i, groups)
            final_send[b] = product(b).astype(jnp.bfloat16)
            final_copy(me, b).start()
            return carry

        lax.fori_loop(0, groups - 1, send_block, 0)
        part[...] = product(me)

        def take_block(i, carry):
            b = lax.rem(me + 1 + i, groups)
            final_copy(b, b).wait_recv()
            part[...] += final_recv[b].astype(jnp.float32)
            return carry

        lax.fori_loop(0, groups - 1, take_block, 0)
        out_ref[...] = offsets[me] * part[...] / points

        def sent_block(i, carry):
            b = lax.rem(me + 1 + i, groups)
            final_copy(me, b).wait_send()
            return carry

        lax.fori_loop(0, groups - 1, sent_block, 0)
    else:
        out_ref[...] = lax.dot_general(gsum[...], enc[...], NT, preferred_element_type=jnp.float32)

    def sent(d, c):
        position = place(d)[0]

        def of_chain(k, d, c):
            @pl.when(position < n - 1)
            def _():
                red_copy(k, d, c).wait_send()

            @pl.when(position > 0)
            def _():
                err_copy(k, d, c).wait_send()

        @pl.when(layer < last)
        def _():
            later_copy(d, c).wait_send()

        on_chains(of_chain, d, c)

        @pl.when(layer > 0)
        def _():
            next_copy(d, c).wait_send()

    each_chunk(sent)


def per_device(shape, context, targets, beyond_targets, positions, donors, encoder, encoder_bias, decoder):
    layers, n, paths = shape
    path = lax.axis_index("path")
    height = positions.shape[0]
    width, feats = encoder.shape[1:]
    cols = decoder.shape[3]
    points = PTS_DEV * paths
    rows = points * height
    groups = n * paths
    block = width // groups
    me = lax.axis_index("feat") * paths + path
    scatter = block % 16 == 0
    if cols % 128:
        targets = lax.dynamic_slice_in_dim(targets, path * cols, cols, 2)
        beyond_targets = lax.dynamic_slice_in_dim(beyond_targets, path * cols, cols, 1)
    bf16, f32 = jnp.bfloat16, jnp.float32
    dma = pltpu.SemaphoreType.DMA
    final = (
        [
            pltpu.VMEM((height, block), f32),
            pltpu.VMEM((groups, height, block), f32),
            pltpu.VMEM((groups, height, block), bf16),
            pltpu.VMEM((groups, height, block), bf16),
        ]
        if scatter
        else [None, None, None, None]
    )
    scratch = [
        pltpu.VMEM((width, feats), bf16),
        pltpu.VMEM((2, feats, cols), bf16),
        pltpu.VMEM((rows, width), bf16),
        pltpu.VMEM((rows, feats), bf16),
        pltpu.VMEM((rows, cols), f32),
        pltpu.VMEM((rows, cols), bf16),
        pltpu.VMEM((rows, cols), bf16),
        pltpu.VMEM((2, rows, cols), bf16),
        pltpu.VMEM((2, rows, cols), bf16),
        pltpu.VMEM((2, rows, cols), bf16),
        pltpu.VMEM((2, rows, cols), bf16),
        pltpu.VMEM((height, feats), bf16),
        *final,
        dma((feats // tile_of(feats, 256),)),
        dma((2,)),
        dma((2, 2, CHUNKS)),
        dma((2, 2, 2, CHUNKS)),
        dma((2, 2, 2, CHUNKS)),
        dma((2, 2, CHUNKS)),
        dma((2, groups)) if scatter else None,
    ]
    kept = [s is not None for s in scratch]

    def body(*refs):
        fixed, given = refs[:9], iter(refs[9:])
        kernel(shape, *fixed, *[next(given) if k else None for k in kept])

    vmem, anywhere = pl.BlockSpec(memory_space=pltpu.VMEM), pl.BlockSpec(memory_space=pl.ANY)
    out = pl.pallas_call(
        body,
        out_shape=jax.ShapeDtypeStruct((height, block if scatter else width), f32),
        in_specs=[vmem] * 6 + [anywhere] * 2,
        out_specs=vmem,
        scratch_shapes=[s for s in scratch if s is not None],
        compiler_params=pltpu.CompilerParams(
            collective_id=0, has_side_effects=True, vmem_limit_bytes=60 * 1024 * 1024
        ),
        name="attribution",
    )(positions[None], donors[None], context, targets, beyond_targets, encoder_bias, encoder, decoder)
    if not scatter:
        quadrature = lax.psum_scatter(out, ("feat", "path"), scatter_dimension=1, tiled=True)
        ctxb = lax.dynamic_slice_in_dim(context[0], me * block, block, 1)
        offset = ctxb[positions].astype(f32) - ctxb[donors].astype(f32)
        out = offset * quadrature / points
    return out[None]


def solution(mesh):
    shape = tuple(mesh.shape[a] for a in ("layer", "feat", "path"))
    placed = (
        P("layer", None, None),
        P("layer", None, None),
        P(),
        P(),
        P(),
        P("layer", None, "feat"),
        P("layer", "feat"),
        P("layer", None, "feat", "path"),
    )
    return jax.shard_map(
        functools.partial(per_device, shape),
        mesh=mesh,
        in_specs=placed,
        out_specs=P("layer", None, ("feat", "path")),
        check_vma=False,
    )
```

```python
import functools

import jax
import jax.numpy as jnp
from jax import lax
from jax.experimental import pallas as pl
from jax.experimental.pallas import tpu as pltpu
from jax.sharding import PartitionSpec as P

PTS_DEV = 4
CHUNKS = 4
SKEW = 6
LEAD = 4
MESH = pl.DeviceIdType.MESH
NT = (((1,), (1,)), ((), ()))


def tile_of(width, most):
    sizes = [t for t in range(128, most + 1, 128) if width % t == 0]
    return sizes[-1] if sizes else width


def aligned(start, size):
    return pl.ds(pl.multiple_of(start, size), size)


def kernel(
    shape, pos_ref, don_ref, ctx_ref, tgt_ref, bey_ref, bias_ref, enc_hbm, dec_hbm, out_ref,
    enc, dec, inputs, codes, own, later, later_in, goal, red_recv, red_send, err, gsum, part, offsets, final_send, final_recv,
    enc_sem, dec_sem, later_sem, red_sem, err_sem, next_sem, final_sem,
):
    layers, n, paths = shape
    layer, z, path = lax.axis_index("layer"), lax.axis_index("feat"), lax.axis_index("path")
    last = layers - 1
    height, tokens = pos_ref.shape[1], ctx_ref.shape[1]
    rows, width = inputs.shape
    feats, cols = codes.shape[1], own.shape[1]
    points = rows // height
    half = rows // 2
    ctile = tile_of(cols, 384)
    ctiles = cols // ctile
    chunk = half // CHUNKS
    chunks = CHUNKS * ctiles
    groups = n * paths
    me = z * paths + path
    scatter = final_send is not None

    barrier = pltpu.get_barrier_semaphore()

    def greet(i, carry):
        other = lax.rem(me + 1 + i, groups)
        pl.semaphore_signal(
            barrier, inc=1, device_id={"feat": other // paths, "path": lax.rem(other, paths)}, device_id_type=MESH
        )
        return carry

    lax.fori_loop(0, groups - 1, greet, 0)

    @pl.when(layer > 0)
    def _():
        pl.semaphore_signal(barrier, inc=1, device_id={"layer": layer - 1}, device_id_type=MESH)

    @pl.when(layer < last)
    def _():
        pl.semaphore_signal(barrier, inc=1, device_id={"layer": layer + 1}, device_id_type=MESH)

    ftile = tile_of(feats, 256)
    ftiles = feats // ftile

    def enc_copy(j):
        return pltpu.make_async_copy(
            enc_hbm.at[0, :, aligned(j * ftile, ftile)], enc.at[:, aligned(j * ftile, ftile)], enc_sem.at[j]
        )

    def dec_copy(k):
        return pltpu.make_async_copy(dec_hbm.at[0, k], dec.at[k], dec_sem.at[k])

    for j in range(ftiles):
        enc_copy(j).start()

    token = lax.broadcasted_iota(jnp.int32, (tokens, height), 0)
    pick_source = (token == pos_ref[...]).astype(jnp.float32).T.astype(jnp.bfloat16)
    pick_donor = (token == don_ref[...]).astype(jnp.float32).T.astype(jnp.bfloat16)

    def pick(which, table):
        return jnp.dot(which, table, preferred_element_type=jnp.float32)

    donor = pick(pick_donor, ctx_ref[0])
    offset = pick(pick_source, ctx_ref[0]) - donor
    for p in range(points):
        inputs[p * height : (p + 1) * height, :] = (donor + ((p + 0.5) / points) * offset).astype(jnp.bfloat16)
    @pl.when(layer == 0)
    def _():
        later_in[...] = jnp.zeros_like(later_in)

    def encode(j, carry):
        enc_copy(j).wait()
        for k in (0, 1):

            @pl.when(j == max(ftiles - LEAD - k, 0))
            def _():
                dec_copy(k).start()

        at = aligned(j * ftile, ftile)
        preact = jnp.dot(inputs[...], enc[:, at], preferred_element_type=jnp.float32) + bias_ref[:, at]
        codes[:, at] = jnp.maximum(preact, 0.0).astype(jnp.bfloat16)
        return carry

    lax.fori_loop(0, ftiles, encode, 0)

    def columns(j):
        return aligned(j * ctile, ctile) if ctiles > 1 else slice(None)

    def decode(k, into, j):
        at = columns(j)
        value = jnp.dot(codes[...], dec[k, :, at], preferred_element_type=jnp.float32)
        into[:, at] = value.astype(into.dtype)

    dec_copy(1).wait()
    pl.semaphore_wait(barrier, groups - 1 + jnp.minimum(layer, 1) + jnp.minimum(last - layer, 1))

    def at_rows(d, c):
        return aligned(d * half + lax.rem(c, CHUNKS) * chunk, chunk), columns(c // CHUNKS)

    def later_copy(d, c):
        at = at_rows(d, c)
        return pltpu.make_async_remote_copy(
            later.at[*at], later_in.at[*at], later_sem.at[0, d, c], later_sem.at[1, d, c],
            device_id={"layer": lax.rem(layer + 1, layers)}, device_id_type=MESH,
        )

    def place(d):
        return (n - 1 - z, z - 1, z + 1) if d == 0 else (z, z + 1, z - 1)

    def wrap(i):
        return lax.rem(i + n, n)

    def red_copy(k, d, c):
        at = at_rows(d, c)
        return pltpu.make_async_remote_copy(
            red_send.at[k, *at], red_recv.at[k, *at], red_sem.at[0, k, d, c], red_sem.at[1, k, d, c],
            device_id={"feat": wrap(place(d)[1])}, device_id_type=MESH,
        )

    def err_copy(k, d, c):
        at = at_rows(d, c)
        return pltpu.make_async_remote_copy(
            err.at[k, *at], err.at[k, *at], err_sem.at[0, k, d, c], err_sem.at[1, k, d, c],
            device_id={"feat": wrap(place(d)[2])}, device_id_type=MESH,
        )

    def next_copy(d, c):
        at = at_rows(d, c)
        return pltpu.make_async_remote_copy(
            err.at[0, *at], err.at[1, *at], next_sem.at[0, d, c], next_sem.at[1, d, c],
            device_id={"layer": lax.rem(layer + last, layers)}, device_id_type=MESH,
        )

    def each_chunk(act):
        def step(c, carry):
            for d in (0, 1):
                act(d, c)
            return carry

        lax.fori_loop(0, chunks, step, 0)

    def fill_goals():
        if tgt_ref.shape[2] == cols:
            goal_at = slice(None)
        else:
            goal_at = aligned(path * cols, cols)
        goals = [pick(pick_source, table).astype(jnp.bfloat16) for table in (tgt_ref[0, :, goal_at], bey_ref[:, goal_at])]
        for p in range(points):
            for k in (0, 1):
                goal[k, p * height : (p + 1) * height, :] = goals[k]

    if scatter:
        block = width // groups
        for b in range(groups):
            offsets[b] = offset[:, b * block : (b + 1) * block]

    def hand_on(k, d, c):
        @pl.when(place(d)[0] > 0)
        def _():
            err_copy(k, d, c).start()

        if k == 0:

            @pl.when(layer > 0)
            def _():
                next_copy(d, c).start()

    def reduce_step(k, d, c):
        at = at_rows(d, c)
        position = place(d)[0]

        def base():
            if k == 1:
                return later[*at].astype(jnp.float32)
            return own[*at] + later_in[*at].astype(jnp.float32)

        if k == 0:

            @pl.when(layer > 0)
            def _():
                later_copy(d, c).wait_recv()

        @pl.when(position == 0)
        def _():
            red_send[k, *at] = base().astype(jnp.bfloat16)
            red_copy(k, d, c).start()

        @pl.when(position > 0)
        def _():
            red_copy(k, d, c).wait_recv()

            @pl.when(position < n - 1)
            def _():
                red_send[k, *at] = (base() + red_recv[k, *at].astype(jnp.float32)).astype(jnp.bfloat16)
                red_copy(k, d, c).start()

            @pl.when(position == n - 1)
            def _():
                rebuilt = base() + red_recv[k, *at].astype(jnp.float32)
                err[k, *at] = (rebuilt - goal[k, *at].astype(jnp.float32)).astype(jnp.bfloat16)
                hand_on(k, d, c)

    def gather_step(k, d, c):
        err_copy(k, d, c).wait_recv()
        hand_on(k, d, c)

    def on_chains(act, d, c):
        act(0, d, c)

        @pl.when(layer == last)
        def _():
            act(1, d, c)

    def chain(t, carry):
        for d in (0, 1):
            position = place(d)[0]
            c = t - SKEW * position

            @pl.when((c >= 0) & (c < chunks))
            def _():
                on_chains(reduce_step, d, c)

            g = t - SKEW * (2 * (n - 1) - position)

            @pl.when((position < n - 1) & (g >= 0) & (g < chunks))
            def _():
                on_chains(gather_step, d, g)

        return carry

    def later_tile(j, carry):
        decode(1, later, j)

        @pl.when(layer < last)
        def _():
            for i in range(CHUNKS):
                for d in (0, 1):
                    later_copy(d, j * CHUNKS + i).start()

        return carry

    def own_tile(j, carry):
        decode(0, own, j)
        lax.fori_loop(j * CHUNKS, (j + 1) * CHUNKS, chain, 0)
        return carry

    lax.fori_loop(0, ctiles, later_tile, 0)
    dec_copy(0).wait()

    goals_late = SKEW * (n - 1) >= chunks
    if not goals_late:
        fill_goals()
    lax.fori_loop(0, ctiles, own_tile, 0)
    if goals_late:
        fill_goals()
    lax.fori_loop(chunks, chunks + SKEW * 2 * (n - 1), chain, 0)

    @pl.when(layer < last)
    def _():
        each_chunk(lambda d, c: next_copy(d, c).wait_recv())

    def grads_step(j, carry):
        at = aligned(j * ftile, ftile)
        grads = lax.dot_general(err[0], dec[0, at, :], NT, preferred_element_type=jnp.float32)
        grads = grads + lax.dot_general(err[1], dec[1, at, :], NT, preferred_element_type=jnp.float32)
        gated = jnp.where(codes[:, at].astype(jnp.float32) > 0, grads, 0.0)
        gsum[:, at] = gated.reshape(points, height, ftile).sum(axis=0).astype(jnp.bfloat16)
        return carry

    lax.fori_loop(0, ftiles, grads_step, 0)

    if scatter:

        def final_copy(sender, target):
            return pltpu.make_async_remote_copy(
                final_send.at[target], final_recv.at[sender], final_sem.at[0, target], final_sem.at[1, sender],
                device_id={"feat": target // paths, "path": lax.rem(target, paths)}, device_id_type=MESH,
            )

        def product(b):
            return lax.dot_general(gsum[...], enc[aligned(b * block, block), :], NT, preferred_element_type=jnp.float32)

        def send_block(i, carry):
            row = i // paths
            b = jnp.where(2 * z < n, n - 1 - row, row) * paths + lax.rem(path + 1 + i, paths)

            @pl.when(b == me)
            def _():
                part[...] = product(b)

            @pl.when(b != me)
            def _():
                final_send[b] = product(b).astype(jnp.bfloat16)
                final_copy(me, b).start()

            return carry

        lax.fori_loop(0, groups, send_block, 0)

        def take_block(i, carry):
            b = lax.rem(me + 1 + i, groups)
            final_copy(b, b).wait_recv()
            part[...] += final_recv[b].astype(jnp.float32)
            return carry

        lax.fori_loop(0, groups - 1, take_block, 0)
        out_ref[...] = offsets[me] * part[...] / points

        def sent_block(i, carry):
            b = lax.rem(me + 1 + i, groups)
            final_copy(me, b).wait_send()
            return carry

        lax.fori_loop(0, groups - 1, sent_block, 0)
    else:
        out_ref[...] = lax.dot_general(gsum[...], enc[...], NT, preferred_element_type=jnp.float32)

    def sent(d, c):
        position = place(d)[0]

        def of_chain(k, d, c):
            @pl.when(position < n - 1)
            def _():
                red_copy(k, d, c).wait_send()

            @pl.when(position > 0)
            def _():
                err_copy(k, d, c).wait_send()

        @pl.when(layer < last)
        def _():
            later_copy(d, c).wait_send()

        on_chains(of_chain, d, c)

        @pl.when(layer > 0)
        def _():
            next_copy(d, c).wait_send()

    each_chunk(sent)


def per_device(shape, context, targets, beyond_targets, positions, donors, encoder, encoder_bias, decoder):
    layers, n, paths = shape
    path = lax.axis_index("path")
    height = positions.shape[0]
    width, feats = encoder.shape[1:]
    cols = decoder.shape[3]
    points = PTS_DEV * paths
    rows = points * height
    groups = n * paths
    block = width // groups
    me = lax.axis_index("feat") * paths + path
    scatter = block % 16 == 0
    if cols % 128:
        targets = lax.dynamic_slice_in_dim(targets, path * cols, cols, 2)
        beyond_targets = lax.dynamic_slice_in_dim(beyond_targets, path * cols, cols, 1)
    bf16, f32 = jnp.bfloat16, jnp.float32
    dma = pltpu.SemaphoreType.DMA
    chunks = CHUNKS * (cols // tile_of(cols, 384))
    final = (
        [
            pltpu.VMEM((height, block), f32),
            pltpu.VMEM((groups, height, block), f32),
            pltpu.VMEM((groups, height, block), bf16),
            pltpu.VMEM((groups, height, block), bf16),
        ]
        if scatter
        else [None, None, None, None]
    )
    scratch = [
        pltpu.VMEM((width, feats), bf16),
        pltpu.VMEM((2, feats, cols), bf16),
        pltpu.VMEM((rows, width), bf16),
        pltpu.VMEM((rows, feats), bf16),
        pltpu.VMEM((rows, cols), f32),
        pltpu.VMEM((rows, cols), bf16),
        pltpu.VMEM((rows, cols), bf16),
        pltpu.VMEM((2, rows, cols), bf16),
        pltpu.VMEM((2, rows, cols), bf16),
        pltpu.VMEM((2, rows, cols), bf16),
        pltpu.VMEM((2, rows, cols), bf16),
        pltpu.VMEM((height, feats), bf16),
        *final,
        dma((feats // tile_of(feats, 256),)),
        dma((2,)),
        dma((2, 2, chunks)),
        dma((2, 2, 2, chunks)),
        dma((2, 2, 2, chunks)),
        dma((2, 2, chunks)),
        dma((2, groups)) if scatter else None,
    ]
    kept = [s is not None for s in scratch]

    def body(*refs):
        fixed, given = refs[:9], iter(refs[9:])
        kernel(shape, *fixed, *[next(given) if k else None for k in kept])

    vmem, anywhere = pl.BlockSpec(memory_space=pltpu.VMEM), pl.BlockSpec(memory_space=pl.ANY)
    out = pl.pallas_call(
        body,
        out_shape=jax.ShapeDtypeStruct((height, block if scatter else width), f32),
        in_specs=[vmem] * 6 + [anywhere] * 2,
        out_specs=vmem,
        scratch_shapes=[s for s in scratch if s is not None],
        compiler_params=pltpu.CompilerParams(
            collective_id=0, has_side_effects=True, vmem_limit_bytes=60 * 1024 * 1024
        ),
        name="attribution",
    )(positions[None], donors[None], context, targets, beyond_targets, encoder_bias, encoder, decoder)
    if not scatter:
        quadrature = lax.psum_scatter(out, ("feat", "path"), scatter_dimension=1, tiled=True)
        ctxb = lax.dynamic_slice_in_dim(context[0], me * block, block, 1)
        offset = ctxb[positions].astype(f32) - ctxb[donors].astype(f32)
        out = offset * quadrature / points
    return out[None]


def solution(mesh):
    shape = tuple(mesh.shape[a] for a in ("layer", "feat", "path"))
    placed = (
        P("layer", None, None),
        P("layer", None, None),
        P(),
        P(),
        P(),
        P("layer", None, "feat"),
        P("layer", "feat"),
        P("layer", None, "feat", "path"),
    )
    return jax.shard_map(
        functools.partial(per_device, shape),
        mesh=mesh,
        in_specs=placed,
        out_specs=P("layer", None, ("feat", "path")),
        check_vma=False,
    )
```
